1024 devices in a mesh: dp: 8 (over y), pipe: 4 (over x), tensor: 32 (over z, core).
Axes of the slice: x: 4, y: 8, z: 16, core: 2. Of those that a mesh axis runs over, the one named last changes fastest.
Arguments:
- queries: bfloat16 [4, 8, 256, 16384], P('pipe', 'dp', None, 'tensor'), may hold values from -120 to 120
- grad_out: bfloat16 [4, 8, 256, 16384], P('pipe', 'dp', None, 'tensor'), may hold values from -6 to 6
- past_keys: bfloat16 [4, 8, 512, 1024], P('pipe', 'dp', 'tensor'), may hold values from -6 to 6
- past_values: bfloat16 [4, 8, 512, 1024], P('pipe', 'dp', 'tensor'), may hold values from -6 to 6
- span_keys: bfloat16 [4, 8, 256, 1024], P('pipe', 'dp', 'tensor'), may hold values from -6 to 6
- span_values: bfloat16 [4, 8, 256, 1024], P('pipe', 'dp', 'tensor'), may hold values from -6 to 6
- normed: bfloat16 [4, 8, 256, 16384], P('pipe', 'dp', None, 'tensor'), may hold values from -6 to 6
- key_weight: bfloat16 [4, 16384, 1024], P('pipe', 'tensor'), may hold values from -0.046875 to 0.046875
- value_weight: bfloat16 [4, 16384, 1024], P('pipe', 'tensor'), may hold values from -0.046875 to 0.046875
- offsets: int32 [4, 8], P('pipe', 'dp'), may hold values from 256 to 512, as said below
Outputs:
- queries_grad: bfloat16 [4, 8, 256, 16384], P('pipe', 'dp', None, 'tensor')
- past_key_grad: float32 [4, 8, 512, 1024], P('pipe', 'dp', 'tensor')
- past_value_grad: float32 [4, 8, 512, 1024], P('pipe', 'dp', 'tensor')
- key_weight_grad: float32 [4, 16384, 1024], P('pipe', 'tensor', 'dp')
- value_weight_grad: float32 [4, 16384, 1024], P('pipe', 'tensor', 'dp')
- section_grad: bfloat16 [4, 8, 256, 16384], P('pipe', 'dp', None, 'tensor')
The draws below stay inside these ranges and needn't reach their ends.
Inputs may be any that keep to these rules, and one draw needn't show every extreme that they name: `offsets`: the number of earlier tokens of that section's sequence that the block's queries see; 256 and 512 are each reached by some section and sequence.
All inputs are finite; a program needn't handle non-finite values.
Results may differ from the reference program's by a relative error of at most 0.014.
The reference program's roundings to bfloat16 on the way count: a program that leaves them out, or rounds other values in their place, can miss the bound.
Values may be sent and summed in bfloat16 or wider, within the bound.
A program may use at most 32 MiB of HBM per device.

```python
import jax
import jax.numpy as jnp
from jax import lax

D = 16384
HD = 128
GROUP = 16
SPAN = 256
PAST = 512
HEADS = 128
KV_HEADS = 8
SECTIONS = 4
SEQS = 8


def draw_queries(key, part):
    shape = (SECTIONS, SEQS, SPAN, HEADS * HD)
    base_key = jax.random.fold_in(key, 21)
    values = jnp.clip(jax.random.normal(base_key, shape, jnp.float32), -6.0, 6.0)
    return values.astype(jnp.bfloat16)


def draw_grad_out(key, part):
    shape = (SECTIONS, SEQS, SPAN, HEADS * HD)
    base_key = jax.random.fold_in(key, 31)
    values = jnp.clip(jax.random.normal(base_key, shape, jnp.float32), -6.0, 6.0)
    return values.astype(jnp.bfloat16)


def draw_offsets(key, part):
    total_count = SECTIONS * SEQS
    value_key, order_key = jax.random.split(jax.random.fold_in(key, 7))
    flat = jax.random.randint(value_key, (total_count,), PAST // 2, PAST + 1, dtype=jnp.int32)
    order = jax.random.permutation(order_key, total_count)
    flat = flat.at[order[0]].set(PAST).at[order[1]].set(PAST // 2)
    return flat.reshape(SECTIONS, SEQS)


def levels(own_key, shape, shards, low, largest):
    loudness = 1.0
    for axis_at, blocks in shards:
        draws = jax.random.uniform(jax.random.fold_in(jax.random.fold_in(own_key, 6), axis_at), (blocks,), jnp.float32, low / len(shards), largest / len(shards))
        loudness = loudness * jnp.repeat(jnp.exp(draws), shape[axis_at] // blocks).reshape((-1,) + (1,) * (len(shape) - 1 - axis_at))
    return loudness


def noise(stream_key, shape, width, limit, shards=(), kind=jnp.bfloat16):
    values = width * jax.random.normal(stream_key, shape, jnp.float32)
    if shards:
        values = values * levels(stream_key, shape, shards, -0.22, 0.18)
    return jnp.clip(values, -limit, limit).astype(kind)


def setup_inputs(seed: int = 0) -> dict:
    arg_keys = jax.random.split(jax.random.key(seed), 11)
    return {
        "queries": draw_queries(jax.random.fold_in(arg_keys[10], 71), 0),
        "grad_out": draw_grad_out(jax.random.fold_in(arg_keys[10], 71), 0),
        "past_keys": noise(arg_keys[2], (SECTIONS, SEQS, PAST, KV_HEADS * HD), 1.0, 6.0, ((0, 4), (1, 8), (2, 32))),
        "past_values": noise(arg_keys[3], (SECTIONS, SEQS, PAST, KV_HEADS * HD), 1.0, 6.0, ((0, 4), (1, 8), (2, 32))),
        "span_keys": noise(arg_keys[4], (SECTIONS, SEQS, SPAN, KV_HEADS * HD), 1.0, 6.0, ((0, 4), (1, 8), (2, 32))),
        "span_values": noise(arg_keys[5], (SECTIONS, SEQS, SPAN, KV_HEADS * HD), 1.0, 6.0, ((0, 4), (1, 8), (2, 32))),
        "normed": noise(arg_keys[6], (SECTIONS, SEQS, SPAN, D), 1.0, 6.0, ((0, 4), (1, 8), (3, 32))),
        "key_weight": noise(arg_keys[7], (SECTIONS, D, KV_HEADS * HD), D ** -0.5, 0.046875, ((0, 4), (1, 32))),
        "value_weight": noise(arg_keys[8], (SECTIONS, D, KV_HEADS * HD), D ** -0.5, 0.046875, ((0, 4), (1, 32))),
        "offsets": draw_offsets(jax.random.fold_in(arg_keys[10], 71), 0),
    }


rope_base = 500000.0
neg_large = -1e30


def rotary_tables(positions):
    half_dim = HD // 2
    freq_index = jnp.arange(half_dim, dtype=jnp.float32)
    inverse_freq = rope_base ** (-2.0 * freq_index / HD)
    angles = positions.astype(jnp.float32)[:, None] * inverse_freq[None, :]
    return jnp.cos(angles), jnp.sin(angles)


def rotate_rows(values, cosine_table, sine_table):
    half_dim = values.shape[1] // 2
    first_half = values[:, :half_dim]
    second_half = values[:, half_dim:]
    return jnp.concatenate([first_half * cosine_table - second_half * sine_table, second_half * cosine_table + first_half * sine_table], axis=1)


def unrotate_rows(gradient, cosine_table, sine_table):
    half_dim = gradient.shape[1] // 2
    first_grad = gradient[:, :half_dim]
    second_grad = gradient[:, half_dim:]
    return jnp.concatenate([first_grad * cosine_table + second_grad * sine_table, second_grad * cosine_table - first_grad * sine_table], axis=1)


def visible_keys(offset):
    row_index = lax.broadcasted_iota(jnp.int32, (SPAN, PAST + SPAN), 0)
    column_index = lax.broadcasted_iota(jnp.int32, (SPAN, PAST + SPAN), 1)
    return jnp.where(column_index < PAST, column_index < offset, column_index - PAST <= row_index)


def attend_backward(query_rows, grad_rows, key_rows, value_rows, offset):
    positions = jnp.concatenate([jnp.arange(PAST, dtype=jnp.int32), offset + jnp.arange(SPAN, dtype=jnp.int32)])
    cosine_table, sine_table = rotary_tables(positions)
    key_turned = rotate_rows(key_rows.astype(jnp.float32), cosine_table, sine_table).astype(jnp.bfloat16)
    scale_factor = HD ** -0.5
    query_float = query_rows.astype(jnp.float32)
    grad_float = grad_rows.astype(jnp.float32)
    key_float = key_turned.astype(jnp.float32)
    value_float = value_rows.astype(jnp.float32)
    scores = jnp.einsum("thd,kd->htk", query_float, key_float) * scale_factor
    visible = visible_keys(offset)[None]
    masked = jnp.where(visible, scores, neg_large)
    row_max = jnp.max(masked, axis=-1, keepdims=True)
    exponent = jnp.where(visible, jnp.exp(masked - row_max), 0.0)
    attention = exponent / jnp.sum(exponent, axis=-1, keepdims=True)
    attention_bf = attention.astype(jnp.bfloat16)
    attention_back = attention_bf.astype(jnp.float32)
    attended = jnp.einsum("htk,kd->thd", attention_back, value_float)
    row_delta = jnp.sum(grad_float * attended, axis=-1)
    grad_attention = jnp.einsum("thd,kd->htk", grad_float, value_float)
    grad_scores = (attention * (grad_attention - row_delta.T[:, :, None])).astype(jnp.bfloat16)
    score_float = grad_scores.astype(jnp.float32)
    query_grad = (jnp.einsum("htk,kd->thd", score_float, key_float) * scale_factor).astype(jnp.bfloat16)
    key_grad = jnp.einsum("htk,thd->kd", score_float, query_float) * scale_factor
    value_grad = jnp.einsum("htk,thd->kd", attention_back, grad_float)
    key_grad = unrotate_rows(key_grad, cosine_table, sine_table)
    return query_grad, key_grad, value_grad


def reference(queries, grad_out, past_keys, past_values, span_keys, span_values, normed, key_weight, value_weight, offsets):
    query_list, past_key_list, past_value_list, input_list = [], [], [], []
    key_weight_list, value_weight_list = [], []
    for section_index in range(SECTIONS):
        key_total = jnp.zeros((D, KV_HEADS * HD), jnp.float32)
        value_total = jnp.zeros((D, KV_HEADS * HD), jnp.float32)
        section_queries, section_past_keys, section_past_values, section_inputs = [], [], [], []
        for replica in range(SEQS):
            offset = offsets[section_index, replica]
            key_all = jnp.concatenate([past_keys[section_index, replica], span_keys[section_index, replica]], axis=0)
            value_all = jnp.concatenate([past_values[section_index, replica], span_values[section_index, replica]], axis=0)
            query_all = queries[section_index, replica]
            grad_all = grad_out[section_index, replica]

            def per_head(head_index, query_all=query_all, grad_all=grad_all, key_all=key_all, value_all=value_all, offset=offset):
                column_start = head_index * (GROUP * HD)
                query_rows = lax.dynamic_slice_in_dim(query_all, column_start, GROUP * HD, 1).reshape(SPAN, GROUP, HD)
                grad_rows = lax.dynamic_slice_in_dim(grad_all, column_start, GROUP * HD, 1).reshape(SPAN, GROUP, HD)
                key_head = lax.dynamic_slice_in_dim(key_all, head_index * HD, HD, 1)
                value_head = lax.dynamic_slice_in_dim(value_all, head_index * HD, HD, 1)
                return attend_backward(query_rows, grad_rows, key_head, value_head, offset)

            query_grad, key_grad, value_grad = lax.map(per_head, jnp.arange(KV_HEADS, dtype=jnp.int32))
            query_grad = jnp.transpose(query_grad, (1, 0, 2, 3)).reshape(SPAN, HEADS * HD)
            key_flat = jnp.transpose(key_grad, (1, 0, 2)).reshape(PAST + SPAN, KV_HEADS * HD)
            value_flat = jnp.transpose(value_grad, (1, 0, 2)).reshape(PAST + SPAN, KV_HEADS * HD)
            span_key = key_flat[PAST:].astype(jnp.bfloat16)
            span_value = value_flat[PAST:].astype(jnp.bfloat16)
            input_grad = jnp.dot(span_key, key_weight[section_index].T, preferred_element_type=jnp.float32)
            input_grad = input_grad + jnp.dot(span_value, value_weight[section_index].T, preferred_element_type=jnp.float32)
            key_part = jnp.dot(normed[section_index, replica].T, span_key, preferred_element_type=jnp.float32)
            value_part = jnp.dot(normed[section_index, replica].T, span_value, preferred_element_type=jnp.float32)
            key_total = key_total + lax.optimization_barrier(key_part.astype(jnp.bfloat16)).astype(jnp.float32)
            value_total = value_total + lax.optimization_barrier(value_part.astype(jnp.bfloat16)).astype(jnp.float32)
            section_queries.append(query_grad)
            section_past_keys.append(key_flat[:PAST])
            section_past_values.append(value_flat[:PAST])
            section_inputs.append(input_grad.astype(jnp.bfloat16))
        query_list.append(jnp.stack(section_queries))
        past_key_list.append(jnp.stack(section_past_keys))
        past_value_list.append(jnp.stack(section_past_values))
        input_list.append(jnp.stack(section_inputs))
        key_weight_list.append(key_total)
        value_weight_list.append(value_total)
    inputs_all = jnp.stack(input_list)
    section_grad = jnp.concatenate([inputs_all[1:], jnp.zeros_like(inputs_all[:1])], axis=0)
    return (jnp.stack(query_list), jnp.stack(past_key_list), jnp.stack(past_value_list), jnp.stack(key_weight_list), jnp.stack(value_weight_list), section_grad)
```

```python
import functools
import math

import jax
import jax.numpy as jnp
from jax import lax
from jax.experimental import pallas as pl
from jax.experimental.pallas import tpu as pltpu
from jax.sharding import PartitionSpec as P

HD = 128
QH = 4
PR = 16
SR = 8
ROPE_BASE = 500000.0
NEG = -1e30
MESH = pl.DeviceIdType.MESH
F32 = jnp.float32
BF16 = jnp.bfloat16

GATHER = {
    16: ((5, -5, 2, -2, 1, -1), ((5, (3, 2, -2, 1, -1)), (-5, (-2, 2, -1, 1)))),
    4: ((1, -1), ((1, (1,)),)),
}


def dot(a, b, ca=1, cb=0):
    return lax.dot_general(a, b, (((ca,), (cb,)), ((), ())), preferred_element_type=F32)


def swap_halves(x):
    return pltpu.roll(x, HD // 2, 1)


def kernel(
    nz, ny, nx,
    off, q_h, go_h, nr_h, pk_h, pv_h, sk_h, sv_h, kw_h, vw_h,
    qg_o, pkg_o, pvg_o, kwg_o, vwg_o, sg_o,
    q, go, nr, pk, pv, sk, sv, kw, vw,
    kvsend, kvrecv, cos, sin, bias, key, key_t, val, q_t, go_t, n_t,
    dk, dv, qg, spart, srecv, ppart, precv, pout, powner, sg_all, dw_all,
    x_lhs, dx, dxb, w_rhs, dwk, dwv, pkg, pvg,
    in_sem, out_sem, kv_s, kv_r, core_s, core_r, grp_s, grp_r, ag_s, ag_r,
    own_s, own_r, ny_s, ny_r, yx_s, yx_r, x_s, x_r,
):
    heads = nz // 2
    past, span = nz * 2 * PR, nz * 2 * SR
    t = lax.axis_index("tensor")
    y = lax.axis_index("dp")
    pipe = lax.axis_index("pipe")
    z, c = t // 2, lax.rem(t, 2)
    head = z // 2
    zp = lax.rem(z, 2)
    zx = z + 1 - 2 * zp

    def at_z(zz, cc):
        return {"tensor": zz * 2 + cc}

    def zmod(d):
        return lax.rem(z + d + nz, nz)

    def ymod(d):
        return lax.rem(y + d + ny, ny)

    def remote(src, dst, ss, rs, dev):
        return pltpu.make_async_remote_copy(
            src_ref=src, dst_ref=dst, send_sem=ss, recv_sem=rs, device_id=dev, device_id_type=MESH
        )

    barrier = pltpu.get_barrier_semaphore()
    peers = [at_z(zmod(d), c) for d in range(1, nz)]
    peers += [at_z(z, 1 - c), at_z(zx, 1 - c)]
    peers += [{"dp": ymod(d)} for d in range(1, ny)]
    if nx > 1:
        peers += [{"pipe": lax.rem(pipe + 1, nx)}, {"pipe": lax.rem(pipe + nx - 1, nx)}]
    for dev in peers:
        pl.semaphore_signal(barrier, inc=1, device_id=dev, device_id_type=MESH)

    loads = {}
    for i, (name, src, dst) in enumerate(
        (("pk", pk_h, pk), ("pv", pv_h, pv), ("sk", sk_h, sk), ("sv", sv_h, sv), ("nr", nr_h, nr),
         ("q", q_h, q), ("go", go_h, go), ("kw", kw_h, kw), ("vw", vw_h, vw))
    ):
        loads[name] = pltpu.make_async_copy(src, dst, in_sem.at[i])
        loads[name].start()
    sends = []

    for name in ("pk", "pv", "sk", "sv"):
        loads[name].wait()
    for h in range(heads):
        cols = slice(h * HD, (h + 1) * HD)
        kvsend[h, 0:PR, :] = pk[:, cols]
        kvsend[h, PR : 2 * PR, :] = pv[:, cols]
        both = jnp.concatenate([sk[:, cols].astype(F32), sv[:, cols].astype(F32)], axis=0)
        kvsend[h, 2 * PR : 2 * PR + 2 * SR, :] = both.astype(BF16)
    kvrecv[c, z] = kvsend[head]

    loads["nr"].wait()
    rows = nr[...].astype(F32).reshape(nz, 2, SR, 512)
    rows = jnp.concatenate([rows[:, 0].reshape(nz * SR, 512), rows[:, 1].reshape(nz * SR, 512)], axis=0)
    n_t[y] = rows.T.astype(BF16)

    offset = off[0, 0]
    logz = int(math.log2(nz))
    ip = lax.broadcasted_iota(jnp.int32, (past, HD), 0)
    pos_p = ((((ip >> 4) & (nz - 1)) * 2 + (ip >> (4 + logz))) << 4) + (ip & 15)
    iu = lax.broadcasted_iota(jnp.int32, (span, HD), 0)
    pos_u = ((((iu >> 3) & (nz - 1)) * 2 + (iu >> (3 + logz))) << 3) + (iu & 7)
    lane = lax.broadcasted_iota(jnp.int32, (1, HD), 1)
    freq = jnp.exp((lane & (HD // 2 - 1)).astype(F32) * (-2.0 / HD * math.log(ROPE_BASE)))
    sign = jnp.where(lane < HD // 2, -1.0, 1.0)
    ang_p = pos_p.astype(F32) * freq
    ang_u = (pos_u + offset).astype(F32) * freq
    cos[0:past, :] = jnp.cos(ang_p)
    sin[0:past, :] = jnp.sin(ang_p) * sign
    cos[past:, :] = jnp.cos(ang_u)
    sin[past:, :] = jnp.sin(ang_u) * sign
    ip = lax.broadcasted_iota(jnp.int32, (past, span), 0)
    pos_p = ((((ip >> 4) & (nz - 1)) * 2 + (ip >> (4 + logz))) << 4) + (ip & 15)
    bias[0:past, :] = jnp.where(pos_p < offset, 0.0, NEG)
    iu = lax.broadcasted_iota(jnp.int32, (span, span), 0)
    pos_u = ((((iu >> 3) & (nz - 1)) * 2 + (iu >> (3 + logz))) << 3) + (iu & 7)
    bias[past:, :] = jnp.where(pos_u <= lax.broadcasted_iota(jnp.int32, (span, span), 1), 0.0, NEG)

    loads["q"].wait()
    loads["go"].wait()
    q_t[...] = q[...].T
    go_t[...] = go[...].T

    pl.semaphore_wait(barrier, len(peers))

    for d in sorted(range(1, nz), key=lambda d: -min(d, nz - d)):
        zd = zmod(d)
        cp = remote(kvsend.at[zd // 2], kvrecv.at[c, z], kv_s.at[d], kv_r.at[d], at_z(zd, c))
        cp.start()
        sends.append(cp)
    plus, minus = ny // 2, ny - 1 - ny // 2

    def pass_input(step):
        for way, last in ((1, plus), (-1, minus)):
            i = 0 if way > 0 else 1
            if 0 < step <= last:
                block = n_t.at[ymod(-way * step)]
                remote(block, block, ny_s.at[i, step], ny_r.at[i, step], {"dp": ymod(way)}).wait_recv()
            if step < last:
                block = n_t.at[ymod(-way * step)]
                cp = remote(block, block, ny_s.at[i, step + 1], ny_r.at[i, step + 1], {"dp": ymod(way)})
                cp.start()
                sends.append(cp)

    pass_input(0)
    for d in range(1, nz):
        slot = kvrecv.at[c, zmod(-d)]
        remote(slot, slot, kv_s.at[d], kv_r.at[d], at_z(zmod(d), c)).wait_recv()
    cp = remote(kvrecv.at[c], kvrecv.at[c], core_s.at[0], core_r.at[0], at_z(z, 1 - c))
    cp.start()
    sends.append(cp)
    pass_input(1)
    remote(kvrecv.at[1 - c], kvrecv.at[1 - c], core_s.at[0], core_r.at[0], at_z(z, 1 - c)).wait_recv()

    half = nz * PR
    shalf = nz * SR
    for cc in range(2):
        kr = kvrecv[cc, :, 0:PR, :].reshape(half, HD).astype(F32)
        lo = cc * half
        kr = kr * cos[lo : lo + half, :] + swap_halves(kr) * sin[lo : lo + half, :]
        key[lo : lo + half, :] = kr.astype(BF16)
        val[lo : lo + half, :] = kvrecv[cc, :, PR : 2 * PR, :].reshape(half, HD)
        both = kvrecv[cc, :, 2 * PR : 2 * PR + 2 * SR, :].astype(F32)
        kr = both[:, 0:SR, :].reshape(shalf, HD)
        lo = past + cc * shalf
        kr = kr * cos[lo : lo + shalf, :] + swap_halves(kr) * sin[lo : lo + shalf, :]
        key[lo : lo + shalf, :] = kr.astype(BF16)
        val[lo : lo + shalf, :] = both[:, SR:, :].reshape(shalf, HD).astype(BF16)
    key_t[...] = key[...].T

    scale = HD**-0.5
    dk[...] = jnp.zeros_like(dk)
    dv[...] = jnp.zeros_like(dv)

    def one_head(h, carry):
        at = pl.ds(pl.multiple_of(h * HD, HD), HD)
        s = dot(key[...], q_t[at, :]) * scale + bias[...]
        e = jnp.exp(s - jnp.max(s, axis=0, keepdims=True))
        a = e * (1.0 / jnp.sum(e, axis=0, keepdims=True))
        ab = a.astype(BF16)
        dp = dot(val[...], go_t[at, :])
        delta = jnp.sum(ab.astype(F32) * dp, axis=0, keepdims=True)
        ds = (a * (dp - delta)).astype(BF16)
        qg[:, at] = (dot(key_t[...], ds) * scale).T.astype(BF16)
        dk[...] += dot(ds, q[:, at])
        dv[...] += dot(ab, go[:, at])
        return carry

    lax.fori_loop(0, QH // 2, one_head, 0)
    pass_input(2)
    lax.fori_loop(QH // 2, QH, one_head, 0)
    out_q = pltpu.make_async_copy(qg, qg_o, out_sem.at[0])
    out_q.start()

    g = dk[...] * scale
    dk[...] = g * cos[...] - swap_halves(g) * sin[...]
    sq, pq = span // 4, past // 4
    for j in range(4):
        for kv, acc in enumerate((dk, dv)):
            spart[j, kv] = acc[past + j * sq : past + (j + 1) * sq, :].astype(BF16)
            ppart[j, kv] = acc[j * pq : (j + 1) * pq, :].astype(BF16)
    mates = ((z, 1 - c, zp), (zx, c, 1 - zp), (zx, 1 - c, 1 - zp))
    for i, part, recv in ((0, spart, srecv), (1, ppart, precv)):
        for k, (mz, mc, mp) in enumerate(mates):
            cp = remote(part.at[mc * 2 + mp], recv.at[k], grp_s.at[i, k], grp_r.at[i, k], at_z(mz, mc))
            cp.start()
            sends.append(cp)
    mine = c * 2 + zp

    def group_sum(i, part, recv):
        for k, (mz, mc, mp) in enumerate(mates):
            remote(recv.at[k], recv.at[k], grp_s.at[i, k], grp_r.at[i, k], at_z(mz, mc)).wait_recv()
        total = part[mine].astype(F32)
        for k in range(3):
            total = total + recv[k].astype(F32)
        return total.astype(BF16)

    sg_all[c, z] = group_sum(0, spart, srecv)

    first, then = GATHER[nz]
    for d in first:
        cp = remote(sg_all.at[c, z], sg_all.at[c, z], ag_s.at[d % nz], ag_r.at[d % nz], at_z(zmod(d), c))
        cp.start()
        sends.append(cp)

    def landed(d):
        slot = sg_all.at[c, zmod(-d)]
        remote(slot, slot, ag_s.at[d % nz], ag_r.at[d % nz], at_z(zmod(d), c)).wait_recv()

    done = set()
    for d, onward in then:
        landed(d)
        done.add(d % nz)
        slot = sg_all.at[c, zmod(-d)]
        for e in onward:
            k = (d + e) % nz
            cp = remote(slot, slot, ag_s.at[k], ag_r.at[k], at_z(zmod(e), c))
            cp.start()
            sends.append(cp)

    total = group_sum(1, ppart, precv)
    for k in range(nz // 2):
        pout[k] = total[:, k * PR : (k + 1) * PR, :]

    def own_copy(k):
        return remote(pout.at[k], powner.at[head], own_s.at[k], own_r.at[head], at_z(zp * (nz // 2) + k, c))

    for k in range(nz // 2):
        there = zp * (nz // 2) + k

        @pl.when(there != z)
        def _():
            own_copy(k).start()

        @pl.when(there == z)
        def _():
            powner[head] = pout[k]

    pass_input(3)
    for k in range(1, nz):
        if k not in done:
            landed(k)
    cp = remote(sg_all.at[c], sg_all.at[c], core_s.at[1], core_r.at[1], at_z(z, 1 - c))
    cp.start()
    sends.append(cp)
    for d in sorted(range(1, ny), key=lambda d: -min(d, ny - d)):
        yd = ymod(d)
        cp = remote(sg_all.at[c, pl.ds(2 * yd, 2)], dw_all.at[c, y], yx_s.at[d], yx_r.at[d], {"dp": yd})
        cp.start()
        sends.append(cp)
    dw_all[c, y] = sg_all[c, pl.ds(2 * y, 2)]

    remote(sg_all.at[1 - c], sg_all.at[1 - c], core_s.at[1], core_r.at[1], at_z(z, 1 - c)).wait_recv()
    for h in range(heads):
        for cc in range(2):
            for p in range(2):
                j = cc * 2 + p
                for kv in range(2):
                    col = (kv * heads + h) * HD
                    x_lhs[j * sq : (j + 1) * sq, col : col + HD] = sg_all[cc, 2 * h + p, kv]
    loads["kw"].wait()
    loads["vw"].wait()
    wide = heads * HD
    dx[...] = dot(x_lhs[:, 0:wide], kw[...], 1, 1)
    total = (dx[...] + dot(x_lhs[:, wide:], vw[...], 1, 1)).reshape(2, nz, SR, 512)
    dxb[...] = jnp.stack([total[0], total[1]], axis=1).reshape(span, 512).astype(BF16)
    x_copy = remote(dxb, sg_o, x_s, x_r, {"pipe": lax.rem(pipe + nx - 1, nx)})
    if nx > 1:

        @pl.when(pipe > 0)
        def _():
            x_copy.start()

    for h in range(heads):
        there = 2 * h + z // (nz // 2)

        @pl.when(there != z)
        def _():
            remote(powner.at[h], powner.at[h], own_s.at[0], own_r.at[h], at_z(there, c)).wait_recv()

    for h in range(heads):
        pkg[:, h * HD : (h + 1) * HD] = powner[h, 0].astype(F32)
        pvg[:, h * HD : (h + 1) * HD] = powner[h, 1].astype(F32)
    out_pk = pltpu.make_async_copy(pkg, pkg_o, out_sem.at[1])
    out_pv = pltpu.make_async_copy(pvg, pvg_o, out_sem.at[2])
    out_pk.start()
    out_pv.start()

    for d in range(1, ny):
        slot = dw_all.at[c, ymod(-d)]
        remote(slot, slot, yx_s.at[d], yx_r.at[d], {"dp": ymod(d)}).wait_recv()
    cp = remote(dw_all.at[c], dw_all.at[c], core_s.at[2], core_r.at[2], at_z(z, 1 - c))
    cp.start()
    sends.append(cp)
    if plus >= 4:
        pass_input(4)
    remote(dw_all.at[1 - c], dw_all.at[1 - c], core_s.at[2], core_r.at[2], at_z(z, 1 - c)).wait_recv()
    dwk[...] = jnp.zeros_like(dwk)
    dwv[...] = jnp.zeros_like(dwv)

    def one_sequence(b, carry):
        for cc in range(2):
            for p in range(2):
                j = cc * 2 + p
                for kv in range(2):
                    w_rhs[j * sq : (j + 1) * sq, kv * HD : (kv + 1) * HD] = dw_all[cc, b, p, kv]
        part = dot(n_t[b], w_rhs[...]).astype(BF16).astype(F32)
        dwk[...] += part[:, 0:HD]
        dwv[...] += part[:, HD:]
        return carry

    lax.fori_loop(0, ny, one_sequence, 0)
    out_wk = pltpu.make_async_copy(dwk, kwg_o, out_sem.at[3])
    out_wv = pltpu.make_async_copy(dwv, vwg_o, out_sem.at[4])
    out_wk.start()
    out_wv.start()

    for k in range(nz // 2):

        @pl.when(zp * (nz // 2) + k != z)
        def _():
            own_copy(k).wait_send()

    for cp in sends:
        cp.wait_send()
    if nx > 1:

        @pl.when(pipe < nx - 1)
        def _():
            x_copy.wait_recv()

        @pl.when(pipe > 0)
        def _():
            x_copy.wait_send()

    @pl.when(pipe == nx - 1)
    def _():
        dxb[...] = jnp.zeros_like(dxb)
        zero = pltpu.make_async_copy(dxb, sg_o, out_sem.at[5])
        zero.start()
        zero.wait()

    for cp in (out_q, out_pk, out_pv, out_wk, out_wv):
        cp.wait()


def on_device(sizes, queries, grad_out, past_keys, past_values, span_keys, span_values, normed,
              key_weight, value_weight, offsets):
    nz, ny, nx = sizes
    heads = nz // 2
    past, span = nz * 2 * PR, nz * 2 * SR
    keys = past + span
    wide = heads * HD
    sq, pq = span // 4, past // 4
    any_ = pl.BlockSpec(memory_space=pl.ANY)
    vm = pltpu.VMEM
    dma = pltpu.SemaphoreType.DMA
    outs = pl.pallas_call(
        functools.partial(kernel, nz, ny, nx),
        name="gqa_backward",
        out_shape=(
            jax.ShapeDtypeStruct((span, QH * HD), BF16),
            jax.ShapeDtypeStruct((PR, wide), F32),
            jax.ShapeDtypeStruct((PR, wide), F32),
            jax.ShapeDtypeStruct((512, HD), F32),
            jax.ShapeDtypeStruct((512, HD), F32),
            jax.ShapeDtypeStruct((span, 512), BF16),
        ),
        in_specs=[pl.BlockSpec(memory_space=pltpu.SMEM)] + [any_] * 9,
        out_specs=(any_,) * 6,
        scratch_shapes=[
            vm((span, 512), BF16), vm((span, 512), BF16), vm((span, 512), BF16),
            vm((PR, wide), BF16), vm((PR, wide), BF16), vm((SR, wide), BF16), vm((SR, wide), BF16),
            vm((512, wide), BF16), vm((512, wide), BF16),
            vm((heads, 48, HD), BF16), vm((2, nz, 48, HD), BF16),
            vm((keys, HD), F32), vm((keys, HD), F32), vm((keys, span), F32),
            vm((keys, HD), BF16), vm((HD, keys), BF16), vm((keys, HD), BF16),
            vm((512, span), BF16), vm((512, span), BF16), vm((ny, 512, span), BF16),
            vm((keys, HD), F32), vm((keys, HD), F32), vm((span, 512), BF16),
            vm((4, 2, sq, HD), BF16), vm((3, 2, sq, HD), BF16),
            vm((4, 2, pq, HD), BF16), vm((3, 2, pq, HD), BF16),
            vm((nz // 2, 2, PR, HD), BF16), vm((heads, 2, PR, HD), BF16),
            vm((2, nz, 2, sq, HD), BF16), vm((2, ny, 2, 2, sq, HD), BF16),
            vm((span, 2 * wide), BF16), vm((span, 512), F32), vm((span, 512), BF16),
            vm((span, 2 * HD), BF16), vm((512, HD), F32), vm((512, HD), F32),
            vm((PR, wide), F32), vm((PR, wide), F32),
            dma((9,)), dma((6,)), dma((nz,)), dma((nz,)), dma((3,)), dma((3,)),
            dma((2, 3)), dma((2, 3)), dma((nz,)), dma((nz,)), dma((nz // 2,)), dma((heads,)),
            dma((2, ny)), dma((2, ny)), dma((ny,)), dma((ny,)), dma, dma,
        ],
        compiler_params=pltpu.CompilerParams(
            collective_id=0, has_side_effects=True, vmem_limit_bytes=48 * 1024 * 1024
        ),
    )(
        offsets, queries[0, 0], grad_out[0, 0], normed[0, 0], past_keys[0, 0], past_values[0, 0],
        span_keys[0, 0], span_values[0, 0], key_weight[0], value_weight[0],
    )
    qg, pkg, pvg, kwg, vwg, sg = outs
    return (qg[None, None], pkg[None, None], pvg[None, None], kwg[None], vwg[None], sg[None, None])


def solution(mesh):
    sizes = (mesh.shape["tensor"] // 2, mesh.shape["dp"], mesh.shape["pipe"])
    rows = P("pipe", "dp", "tensor", None)
    cols = P("pipe", "dp", None, "tensor")
    weight = P("pipe", "tensor", None)
    return jax.shard_map(
        functools.partial(on_device, sizes),
        mesh=mesh,
        in_specs=(cols, cols, rows, rows, rows, rows, cols, weight, weight, P("pipe", "dp")),
        out_specs=(cols, rows, rows, P("pipe", "tensor", "dp"), P("pipe", "tensor", "dp"), cols),
        check_vma=False,
    )
```

```python
import functools
import math

import jax
import jax.numpy as jnp
from jax import lax
from jax.experimental import pallas as pl
from jax.experimental.pallas import tpu as pltpu
from jax.sharding import PartitionSpec as P

HD = 128
QH = 4
PR = 16
SR = 8
ROPE_BASE = 500000.0
NEG = -1e30
MESH = pl.DeviceIdType.MESH
F32 = jnp.float32
BF16 = jnp.bfloat16

GATHER = {
    16: ((5, -5, 2, -2, 1, -1), ((5, (3, 2, -2, 1, -1)), (-5, (-2, 2, -1, 1)))),
    4: ((1, -1), ((1, (1,)),)),
}


def dot(a, b, ca=1, cb=0):
    return lax.dot_general(a, b, (((ca,), (cb,)), ((), ())), preferred_element_type=F32)


def swap_halves(x):
    return pltpu.roll(x, HD // 2, 1)


def kernel(
    nz, ny, nx,
    off, q_h, go_h, nr_h, pk_h, pv_h, sk_h, sv_h, kw_h, vw_h,
    qg, pkg, pvg, dwk, dwv, sg_o,
    q, go, nr, pk, pv, sk, sv, kw, vw,
    kvsend, kvrecv, cos, sin, bias, key, key_t, val, q_t, go_t, n_t,
    dk, dv, spart, srecv, ppart, precv, pout, powner, sg_all, dw_all,
    x_lhs, dx, dxb, w_rhs,
    in_sem, kv_s, kv_r, core_s, core_r, grp_s, grp_r, ag_s, ag_r,
    own_s, own_r, ny_s, ny_r, yx_s, yx_r, yc_s, yc_r, x_s, x_r,
):
    heads = nz // 2
    past, span = nz * 2 * PR, nz * 2 * SR
    t = lax.axis_index("tensor")
    y = lax.axis_index("dp")
    pipe = lax.axis_index("pipe")
    z, c = t // 2, lax.rem(t, 2)
    head = z // 2
    zp = lax.rem(z, 2)
    zx = z + 1 - 2 * zp

    def at_z(zz, cc):
        return {"tensor": zz * 2 + cc}

    def zmod(d):
        return lax.rem(z + d + nz, nz)

    def ymod(d):
        return lax.rem(y + d + ny, ny)

    def remote(src, dst, ss, rs, dev):
        return pltpu.make_async_remote_copy(
            src_ref=src, dst_ref=dst, send_sem=ss, recv_sem=rs, device_id=dev, device_id_type=MESH
        )

    barrier = pltpu.get_barrier_semaphore()
    peers = [at_z(zmod(d), c) for d in range(1, nz)]
    peers += [at_z(z, 1 - c), at_z(zx, 1 - c)]
    peers += [{"dp": ymod(d)} for d in range(1, ny)]
    if nx > 1:
        peers += [{"pipe": lax.rem(pipe + 1, nx)}, {"pipe": lax.rem(pipe + nx - 1, nx)}]
    for dev in peers:
        pl.semaphore_signal(barrier, inc=1, device_id=dev, device_id_type=MESH)

    loads = {}
    for i, (name, src, dst) in enumerate(
        (("pk", pk_h, pk), ("pv", pv_h, pv), ("sk", sk_h, sk), ("sv", sv_h, sv), ("nr", nr_h, nr),
         ("q", q_h, q), ("go", go_h, go), ("kw", kw_h, kw), ("vw", vw_h, vw))
    ):
        loads[name] = pltpu.make_async_copy(src, dst, in_sem.at[i])
        loads[name].start()
    sends = []

    for name in ("pk", "pv", "sk", "sv"):
        loads[name].wait()
    for h in range(heads):
        cols = slice(h * HD, (h + 1) * HD)
        kvsend[h, 0:PR, :] = pk[:, cols]
        kvsend[h, PR : 2 * PR, :] = pv[:, cols]
        both = jnp.concatenate([sk[:, cols].astype(F32), sv[:, cols].astype(F32)], axis=0)
        kvsend[h, 2 * PR : 2 * PR + 2 * SR, :] = both.astype(BF16)
    kvrecv[c, z] = kvsend[head]

    pl.semaphore_wait(barrier, len(peers))

    for d in sorted(range(1, nz), key=lambda d: -min(d, nz - d)):
        zd = zmod(d)
        cp = remote(kvsend.at[zd // 2], kvrecv.at[c, z], kv_s.at[d], kv_r.at[d], at_z(zd, c))
        cp.start()
        sends.append(cp)
    loads["nr"].wait()
    rows = nr[...].astype(F32).reshape(nz, 2, SR, 512)
    e = nz // 4
    pieces = [
        rows[p * 2 * e + hf * e : p * 2 * e + (hf + 1) * e, cc].reshape(e * SR, 512)
        for hf in range(2) for cc in range(2) for p in range(2)
    ]
    rows = jnp.concatenate(pieces, axis=0)
    n_t[y] = rows.T.astype(BF16)

    plus, minus = ny // 2, ny - 1 - ny // 2

    def pass_input(step):
        for way, last in ((1, plus), (-1, minus)):
            i = 0 if way > 0 else 1
            if 0 < step <= last:
                block = n_t.at[ymod(-way * step)]
                remote(block, block, ny_s.at[i, step], ny_r.at[i, step], {"dp": ymod(way)}).wait_recv()
            if step < last:
                block = n_t.at[ymod(-way * step)]
                cp = remote(block, block, ny_s.at[i, step + 1], ny_r.at[i, step + 1], {"dp": ymod(way)})
                cp.start()
                sends.append(cp)

    pass_input(0)

    offset = off[0, 0]
    logz = int(math.log2(nz))
    ip = lax.broadcasted_iota(jnp.int32, (past, HD), 0)
    pos_p = ((((ip >> 4) & (nz - 1)) * 2 + (ip >> (4 + logz))) << 4) + (ip & 15)
    iu = lax.broadcasted_iota(jnp.int32, (span, HD), 0)
    pos_u = ((((iu >> 3) & (nz - 1)) * 2 + (iu >> (3 + logz))) << 3) + (iu & 7)
    lane = lax.broadcasted_iota(jnp.int32, (1, HD), 1)
    freq = jnp.exp((lane & (HD // 2 - 1)).astype(F32) * (-2.0 / HD * math.log(ROPE_BASE)))
    sign = jnp.where(lane < HD // 2, -1.0, 1.0)
    ang_p = pos_p.astype(F32) * freq
    ang_u = (pos_u + offset).astype(F32) * freq
    cos[0:past, :] = jnp.cos(ang_p)
    sin[0:past, :] = jnp.sin(ang_p) * sign
    cos[past:, :] = jnp.cos(ang_u)
    sin[past:, :] = jnp.sin(ang_u) * sign
    ip = lax.broadcasted_iota(jnp.int32, (past, span), 0)
    pos_p = ((((ip >> 4) & (nz - 1)) * 2 + (ip >> (4 + logz))) << 4) + (ip & 15)
    bias[0:past, :] = jnp.where(pos_p < offset, 0.0, NEG)
    iu = lax.broadcasted_iota(jnp.int32, (span, span), 0)
    pos_u = ((((iu >> 3) & (nz - 1)) * 2 + (iu >> (3 + logz))) << 3) + (iu & 7)
    bias[past:, :] = jnp.where(pos_u <= lax.broadcasted_iota(jnp.int32, (span, span), 1), 0.0, NEG)

    loads["q"].wait()
    loads["go"].wait()
    q_t[...] = q[...].T
    go_t[...] = go[...].T

    for d in range(1, nz):
        slot = kvrecv.at[c, zmod(-d)]
        remote(slot, slot, kv_s.at[d], kv_r.at[d], at_z(zmod(d), c)).wait_recv()
    cp = remote(kvrecv.at[c], kvrecv.at[c], core_s.at[0, 0], core_r.at[0, 0], at_z(z, 1 - c))
    cp.start()
    sends.append(cp)
    pass_input(1)
    remote(kvrecv.at[1 - c], kvrecv.at[1 - c], core_s.at[0, 0], core_r.at[0, 0], at_z(z, 1 - c)).wait_recv()

    half = nz * PR
    shalf = nz * SR
    for cc in range(2):
        kr = kvrecv[cc, :, 0:PR, :].reshape(half, HD).astype(F32)
        lo = cc * half
        kr = kr * cos[lo : lo + half, :] + swap_halves(kr) * sin[lo : lo + half, :]
        key[lo : lo + half, :] = kr.astype(BF16)
        val[lo : lo + half, :] = kvrecv[cc, :, PR : 2 * PR, :].reshape(half, HD)
        both = kvrecv[cc, :, 2 * PR : 2 * PR + 2 * SR, :].astype(F32)
        kr = both[:, 0:SR, :].reshape(shalf, HD)
        lo = past + cc * shalf
        kr = kr * cos[lo : lo + shalf, :] + swap_halves(kr) * sin[lo : lo + shalf, :]
        key[lo : lo + shalf, :] = kr.astype(BF16)
        val[lo : lo + shalf, :] = both[:, SR:, :].reshape(shalf, HD).astype(BF16)
    key_t[...] = key[...].T

    scale = HD**-0.5
    dk[...] = jnp.zeros_like(dk)
    dv[...] = jnp.zeros_like(dv)

    def one_head(h, carry):
        at = pl.ds(pl.multiple_of(h * HD, HD), HD)
        s = dot(key[...], q_t[at, :]) * scale + bias[...]
        e = jnp.exp(s - jnp.max(s, axis=0, keepdims=True))
        a = e * (1.0 / jnp.sum(e, axis=0, keepdims=True))
        ab = a.astype(BF16)
        dp = dot(val[...], go_t[at, :])
        delta = jnp.sum(ab.astype(F32) * dp, axis=0, keepdims=True)
        ds = (a * (dp - delta)).astype(BF16)
        qg[:, at] = (dot(key_t[...], ds) * scale).T.astype(BF16)
        dk[...] += dot(ds, q[:, at])
        dv[...] += dot(ab, go[:, at])
        return carry

    lax.fori_loop(0, QH, one_head, 0)

    g = dk[...] * scale
    dk[...] = g * cos[...] - swap_halves(g) * sin[...]
    sq, pq = span // 8, past // 4
    for j in range(4):
        for kv, acc in enumerate((dk, dv)):
            for hf in range(2):
                at = past + (2 * j + hf) * sq
                spart[hf, j, kv] = acc[at : at + sq, :].astype(BF16)
    mates = ((z, 1 - c, zp), (zx, c, 1 - zp), (zx, 1 - c, 1 - zp))

    def to_mates(i, part, recv):
        for k, (mz, mc, mp) in enumerate(mates):
            cp = remote(part.at[mc * 2 + mp], recv.at[k], grp_s.at[i, k], grp_r.at[i, k], at_z(mz, mc))
            cp.start()
            sends.append(cp)

    mine = c * 2 + zp

    def group_sum(i, part, recv):
        for k, (mz, mc, mp) in enumerate(mates):
            remote(recv.at[k], recv.at[k], grp_s.at[i, k], grp_r.at[i, k], at_z(mz, mc)).wait_recv()
        total = part[mine].astype(F32)
        for k in range(3):
            total = total + recv[k].astype(F32)
        return total.astype(BF16)

    for hf in range(2):
        to_mates(hf, spart.at[hf], srecv.at[hf])
    for j in range(4):
        for kv, acc in enumerate((dk, dv)):
            ppart[j, kv] = acc[j * pq : (j + 1) * pq, :].astype(BF16)
    pass_input(2)

    first, then = GATHER[nz]

    def ring(hf, d, e):
        slot, k = sg_all.at[hf, c, zmod(-d)], (d + e) % nz
        cp = remote(slot, slot, ag_s.at[hf, k], ag_r.at[hf, k], at_z(zmod(e), c))
        cp.start()
        sends.append(cp)

    def landed(hf, d):
        slot = sg_all.at[hf, c, zmod(-d)]
        remote(slot, slot, ag_s.at[hf, d], ag_r.at[hf, d], at_z(zmod(d), c)).wait_recv()

    def over_y(hf, d):
        zo = zmod(-d)
        src, dst = sg_all.at[hf, c, zo], dw_all.at[hf, c, y, lax.rem(zo, 2)]
        return zo // 2, remote(src, dst, yx_s.at[hf, d], yx_r.at[hf, y, lax.rem(zo, 2)], {"dp": zo // 2})

    def pass_on(hf, d):
        zo = zmod(-d)
        slot = sg_all.at[hf, c, zo]
        cp = remote(slot, slot, core_s.at[1 + hf, d], core_r.at[1 + hf, d], at_z(z, 1 - c))
        cp.start()
        sends.append(cp)
        there, yc = over_y(hf, d)

        @pl.when(there != y)
        def _():
            yc.start()

        @pl.when(there == y)
        def _():
            dw_all[hf, c, y, lax.rem(zo, 2)] = sg_all[hf, c, zo]

    for hf in range(2):
        sg_all[hf, c, z] = group_sum(hf, spart.at[hf], srecv.at[hf])
        for d in first:
            ring(hf, 0, d)
        pass_on(hf, 0)
    to_mates(2, ppart, precv)
    done = []
    for hf in range(2):
        for d, onward in then:
            landed(hf, d % nz)
            for e in onward:
                ring(hf, d % nz, e)
            pass_on(hf, d % nz)
            done.append((hf, d % nz))
    pass_input(3)
    for hf in range(2):
        for d in first:
            if (hf, d % nz) not in done:
                landed(hf, d % nz)
                pass_on(hf, d % nz)
                done.append((hf, d % nz))

    total = group_sum(2, ppart, precv)
    for k in range(nz // 2):
        pout[k] = total[:, k * PR : (k + 1) * PR, :]

    def own_copy(k):
        return remote(pout.at[k], powner.at[head], own_s.at[k], own_r.at[head], at_z(zp * (nz // 2) + k, c))

    for k in range(nz // 2):
        there = zp * (nz // 2) + k

        @pl.when(there != z)
        def _():
            own_copy(k).start()

        @pl.when(there == z)
        def _():
            powner[head] = pout[k]

    loads["kw"].wait()
    loads["vw"].wait()
    wide = heads * HD
    x_copies = []
    order = sorted(range(1, nz), key=lambda d: min(d, nz - d))
    for hf in range(2):
        for d in order:
            if (hf, d) not in done:
                landed(hf, d)
                pass_on(hf, d)
        for d in range(nz):
            slot = sg_all.at[hf, 1 - c, zmod(-d)]
            remote(slot, slot, core_s.at[1 + hf, d], core_r.at[1 + hf, d], at_z(z, 1 - c)).wait_recv()
        for h in range(heads):
            for cc in range(2):
                for p in range(2):
                    at = (cc * 2 + p) * sq
                    for kv in range(2):
                        col = (kv * heads + h) * HD
                        x_lhs[hf, at : at + sq, col : col + HD] = sg_all[hf, cc, 2 * h + p, kv]
        dx[...] = dot(x_lhs[hf, :, 0:wide], kw[...], 1, 1)
        total = (dx[...] + dot(x_lhs[hf, :, wide:], vw[...], 1, 1)).reshape(2, nz // 2, SR, 512)
        total = jnp.stack([total[0], total[1]], axis=1).reshape(2, span // 4, 512).astype(BF16)
        dxb[hf] = total
        x_copy = remote(dxb.at[hf], sg_o.at[:, hf], x_s.at[hf], x_r.at[hf], {"pipe": lax.rem(pipe + nx - 1, nx)})
        x_copies.append(x_copy)
        if nx > 1:
            pl.when(pipe > 0)(x_copy.start)

    for h in range(heads):
        there = 2 * h + z // (nz // 2)

        @pl.when(there != z)
        def _():
            remote(powner.at[h], powner.at[h], own_s.at[0], own_r.at[h], at_z(there, c)).wait_recv()

    for h in range(heads):
        pkg[:, h * HD : (h + 1) * HD] = powner[h, 0].astype(F32)
        pvg[:, h * HD : (h + 1) * HD] = powner[h, 1].astype(F32)

    for hf in range(2):
        for d in range(ny):
            b = ymod(-d)
            slot = dw_all.at[hf, c, b]
            if d > 0:
                for p in range(2):
                    part = slot.at[p]
                    remote(part, part, yx_s.at[hf, 0], yx_r.at[hf, b, p], {"dp": ymod(d)}).wait_recv()
            cp = remote(slot, slot, yc_s.at[hf, d], yc_r.at[hf, d], at_z(z, 1 - c))
            cp.start()
            sends.append(cp)
    if plus >= 4:
        pass_input(4)
    for hf in range(2):
        for d in range(ny):
            slot = dw_all.at[hf, 1 - c, ymod(-d)]
            remote(slot, slot, yc_s.at[hf, d], yc_r.at[hf, d], at_z(z, 1 - c)).wait_recv()
    dwk[...] = jnp.zeros_like(dwk)
    dwv[...] = jnp.zeros_like(dwv)

    def one_sequence(b, carry):
        for hf in range(2):
            for cc in range(2):
                for p in range(2):
                    at = (hf * 4 + cc * 2 + p) * sq
                    for kv in range(2):
                        w_rhs[at : at + sq, kv * HD : (kv + 1) * HD] = dw_all[hf, cc, b, p, kv]
        part = dot(n_t[b], w_rhs[...]).astype(BF16).astype(F32)
        dwk[...] += part[:, 0:HD]
        dwv[...] += part[:, HD:]
        return carry

    lax.fori_loop(0, ny, one_sequence, 0)

    for hf in range(2):
        for d in range(nz):
            there, yc = over_y(hf, d)
            pl.when(there != y)(yc.wait_send)
    for k in range(nz // 2):

        @pl.when(zp * (nz // 2) + k != z)
        def _():
            own_copy(k).wait_send()

    for cp in sends:
        cp.wait_send()
    if nx > 1:
        for x_copy in x_copies:
            pl.when(pipe < nx - 1)(x_copy.wait_recv)
            pl.when(pipe > 0)(x_copy.wait_send)

    @pl.when(pipe == nx - 1)
    def _():
        sg_o[...] = jnp.zeros_like(sg_o)


def finish(*refs):
    copies = [pltpu.make_async_copy(a, b, refs[12].at[i]) for i, (a, b) in enumerate(zip(refs[:6], refs[6:12]))]
    for cp in copies:
        cp.start()
    for cp in copies:
        cp.wait()


def on_device(sizes, queries, grad_out, past_keys, past_values, span_keys, span_values, normed,
              key_weight, value_weight, offsets):
    nz, ny, nx = sizes
    heads = nz // 2
    past, span = nz * 2 * PR, nz * 2 * SR
    keys = past + span
    wide = heads * HD
    sq, pq = span // 8, past // 4
    any_ = pl.BlockSpec(memory_space=pltpu.HBM)
    vm = pltpu.VMEM
    dma = pltpu.SemaphoreType.DMA
    outs = pl.pallas_call(
        functools.partial(kernel, nz, ny, nx),
        name="gqa_backward",
        out_shape=(
            vm((span, QH * HD), BF16), vm((PR, wide), F32), vm((PR, wide), F32),
            vm((512, HD), F32), vm((512, HD), F32), vm((2, 2, span // 4, 512), BF16),
        ),
        in_specs=[pl.BlockSpec(memory_space=pltpu.SMEM)] + [any_] * 9,
        out_specs=(pl.BlockSpec(memory_space=pltpu.VMEM),) * 6,
        scratch_shapes=[
            vm((span, 512), BF16), vm((span, 512), BF16), vm((span, 512), BF16),
            vm((PR, wide), BF16), vm((PR, wide), BF16), vm((SR, wide), BF16), vm((SR, wide), BF16),
            vm((512, wide), BF16), vm((512, wide), BF16),
            vm((heads, 48, HD), BF16), vm((2, nz, 48, HD), BF16),
            vm((keys, HD), F32), vm((keys, HD), F32), vm((keys, span), F32),
            vm((keys, HD), BF16), vm((HD, keys), BF16), vm((keys, HD), BF16),
            vm((512, span), BF16), vm((512, span), BF16), vm((ny, 512, span), BF16),
            vm((keys, HD), F32), vm((keys, HD), F32),
            vm((2, 4, 2, sq, HD), BF16), vm((2, 3, 2, sq, HD), BF16),
            vm((4, 2, pq, HD), BF16), vm((3, 2, pq, HD), BF16),
            vm((nz // 2, 2, PR, HD), BF16), vm((heads, 2, PR, HD), BF16),
            vm((2, 2, nz, 2, sq, HD), BF16), vm((2, 2, ny, 2, 2, sq, HD), BF16),
            vm((2, span // 2, 2 * wide), BF16), vm((span // 2, 512), F32), vm((2, 2, span // 4, 512), BF16),
            vm((span, 2 * HD), BF16),
            dma((9,)), dma((nz,)), dma((nz,)), dma((3, nz)), dma((3, nz)),
            dma((3, 3)), dma((3, 3)), dma((2, nz)), dma((2, nz)), dma((nz // 2,)), dma((heads,)),
            dma((2, ny)), dma((2, ny)), dma((2, nz)), dma((2, ny, 2)), dma((2, ny)), dma((2, ny)), dma((2,)), dma((2,)),
        ],
        compiler_params=pltpu.CompilerParams(
            collective_id=0, has_side_effects=True, vmem_limit_bytes=67043328 - (3 << 19)
        ),
    )(
        offsets, queries[0, 0], grad_out[0, 0], normed[0, 0], past_keys[0, 0], past_values[0, 0],
        span_keys[0, 0], span_values[0, 0], key_weight[0], value_weight[0],
    )
    outs = pl.pallas_call(
        finish,
        name="finish",
        out_shape=tuple(jax.ShapeDtypeStruct(o.shape, o.dtype) for o in outs),
        in_specs=[pl.BlockSpec(memory_space=pl.ANY)] * 6,
        out_specs=(pl.BlockSpec(memory_space=pltpu.HBM),) * 6,
        scratch_shapes=[dma((6,))],
        compiler_params=pltpu.CompilerParams(vmem_limit_bytes=1 << 20),
    )(*outs)
    qg, pkg, pvg, kwg, vwg, sg = outs
    return (qg[None, None], pkg[None, None], pvg[None, None], kwg[None], vwg[None], sg.reshape(1, 1, span, 512))


def solution(mesh):
    sizes = (mesh.shape["tensor"] // 2, mesh.shape["dp"], mesh.shape["pipe"])
    rows = P("pipe", "dp", "tensor", None)
    cols = P("pipe", "dp", None, "tensor")
    weight = P("pipe", "tensor", None)
    return jax.shard_map(
        functools.partial(on_device, sizes),
        mesh=mesh,
        in_specs=(cols, cols, rows, rows, rows, rows, cols, weight, weight, P("pipe", "dp")),
        out_specs=(cols, rows, rows, P("pipe", "tensor", "dp"), P("pipe", "tensor", "dp"), cols),
        check_vma=False,
    )
```

```python
import functools
import math

import jax
import jax.numpy as jnp
from jax import lax
from jax.experimental import pallas as pl
from jax.experimental.pallas import tpu as pltpu
from jax.sharding import PartitionSpec as P

HD = 128
QH = 4
PR = 16
SR = 8
ROPE_BASE = 500000.0
NEG = -1e30
MESH = pl.DeviceIdType.MESH
F32 = jnp.float32
BF16 = jnp.bfloat16

GATHER = {
    16: ((5, -5, 2, -2, 1, -1), ((5, (3, 2, -2, 1, -1)), (-5, (-2, 2, -1, 1)))),
    4: ((1, -1), ((1, (1,)),)),
}


def dot(a, b, ca=1, cb=0):
    return lax.dot_general(a, b, (((ca,), (cb,)), ((), ())), preferred_element_type=F32)


def swap_halves(x):
    return pltpu.roll(x, HD // 2, 1)


def kernel(
    nz, ny, nx,
    off, q_h, go_h, nr_h, pk_h, pv_h, sk_h, sv_h, kw_h, vw_h,
    qg, pkg, pvg, dwk, dwv, sg_o,
    q, go, nr, pk, pv, sk, sv, kw, vw,
    kvsend, kvrecv, cos, sin, bias, key, key_t, val, q_t, go_t, n_t,
    dk, dv, spart, srecv, ppart, precv, pout, powner, sg_all, dw_all,
    x_lhs, dx, dxb, w_rhs,
    in_sem, kv_s, kv_r, core_s, core_r, grp_s, grp_r, ag_s, ag_r,
    own_s, own_r, ny_s, ny_r, yx_s, yx_r, yc_s, yc_r, x_s, x_r,
):
    heads = nz // 2
    past, span = nz * 2 * PR, nz * 2 * SR
    t = lax.axis_index("tensor")
    y = lax.axis_index("dp")
    pipe = lax.axis_index("pipe")
    z, c = t // 2, lax.rem(t, 2)
    head = z // 2
    zp = lax.rem(z, 2)
    zx = z + 1 - 2 * zp

    def at_z(zz, cc):
        return {"tensor": zz * 2 + cc}

    def zmod(d):
        return lax.rem(z + d + nz, nz)

    def ymod(d):
        return lax.rem(y + d + ny, ny)

    def remote(src, dst, ss, rs, dev):
        return pltpu.make_async_remote_copy(
            src_ref=src, dst_ref=dst, send_sem=ss, recv_sem=rs, device_id=dev, device_id_type=MESH
        )

    barrier = pltpu.get_barrier_semaphore()
    peers = [at_z(zmod(d), c) for d in range(1, nz)]
    peers += [at_z(z, 1 - c), at_z(zx, 1 - c)]
    peers += [{"dp": ymod(d)} for d in range(1, ny)]
    if nx > 1:
        peers += [{"pipe": lax.rem(pipe + 1, nx)}, {"pipe": lax.rem(pipe + nx - 1, nx)}]
    for dev in peers:
        pl.semaphore_signal(barrier, inc=1, device_id=dev, device_id_type=MESH)

    loads = {}
    for i, (name, src, dst) in enumerate(
        (("pk", pk_h, pk), ("pv", pv_h, pv), ("sk", sk_h, sk), ("sv", sv_h, sv), ("nr", nr_h, nr),
         ("q", q_h, q), ("go", go_h, go), ("kw", kw_h, kw), ("vw", vw_h, vw))
    ):
        loads[name] = pltpu.make_async_copy(src, dst, in_sem.at[i])
        loads[name].start()
    sends = []

    for name in ("pk", "pv", "sk", "sv"):
        loads[name].wait()
    for h in range(heads):
        cols = slice(h * HD, (h + 1) * HD)
        kvsend[h, 0:PR, :] = pk[:, cols]
        kvsend[h, PR : 2 * PR, :] = pv[:, cols]
        both = jnp.concatenate([sk[:, cols].astype(F32), sv[:, cols].astype(F32)], axis=0)
        kvsend[h, 2 * PR : 2 * PR + 2 * SR, :] = both.astype(BF16)
    kvrecv[c, z] = kvsend[head]

    pl.semaphore_wait(barrier, len(peers))

    for d in sorted(range(1, nz), key=lambda d: -min(d, nz - d)):
        zd = zmod(d)
        cp = remote(kvsend.at[zd // 2], kvrecv.at[c, z], kv_s.at[d], kv_r.at[d], at_z(zd, c))
        cp.start()
        sends.append(cp)
    loads["nr"].wait()
    rows = nr[...].astype(F32).reshape(nz, 2, SR, 512)
    e = nz // 4
    pieces = [
        rows[p * 2 * e + hf * e : p * 2 * e + (hf + 1) * e, cc].reshape(e * SR, 512)
        for hf in range(2) for cc in range(2) for p in range(2)
    ]
    rows = jnp.concatenate(pieces, axis=0)
    n_t[y] = rows.T.astype(BF16)


    def pass_input(step):
        for i, way in enumerate((1, -1)):

            def block(k):
                o = ymod(-way * k)
                return n_t.at[o, i * 256 : (i + 1) * 256] if 2 * k == ny else n_t.at[o]

            def move(src, k):
                return remote(src, src, ny_s.at[i, k], ny_r.at[i, k], {"dp": ymod(way)})

            if step > 0:
                move(block(step), step).wait_recv()
            if 2 * step < ny:
                o = ymod(-way * step)
                src = n_t.at[o, i * 256 : (i + 1) * 256] if 2 * (step + 1) == ny else n_t.at[o]
                cp = move(src, step + 1)
                cp.start()
                sends.append(cp)

    pass_input(0)

    offset = off[0, 0]
    logz = int(math.log2(nz))
    ip = lax.broadcasted_iota(jnp.int32, (past, HD), 0)
    pos_p = ((((ip >> 4) & (nz - 1)) * 2 + (ip >> (4 + logz))) << 4) + (ip & 15)
    iu = lax.broadcasted_iota(jnp.int32, (span, HD), 0)
    pos_u = ((((iu >> 3) & (nz - 1)) * 2 + (iu >> (3 + logz))) << 3) + (iu & 7)
    lane = lax.broadcasted_iota(jnp.int32, (1, HD), 1)
    freq = jnp.exp((lane & (HD // 2 - 1)).astype(F32) * (-2.0 / HD * math.log(ROPE_BASE)))
    sign = jnp.where(lane < HD // 2, -1.0, 1.0)
    ang_p = pos_p.astype(F32) * freq
    ang_u = (pos_u + offset).astype(F32) * freq
    cos[0:past, :] = jnp.cos(ang_p)
    sin[0:past, :] = jnp.sin(ang_p) * sign
    cos[past:, :] = jnp.cos(ang_u)
    sin[past:, :] = jnp.sin(ang_u) * sign
    ip = lax.broadcasted_iota(jnp.int32, (past, span), 0)
    pos_p = ((((ip >> 4) & (nz - 1)) * 2 + (ip >> (4 + logz))) << 4) + (ip & 15)
    bias[0:past, :] = jnp.where(pos_p < offset, 0.0, NEG)
    iu = lax.broadcasted_iota(jnp.int32, (span, span), 0)
    pos_u = ((((iu >> 3) & (nz - 1)) * 2 + (iu >> (3 + logz))) << 3) + (iu & 7)
    bias[past:, :] = jnp.where(pos_u <= lax.broadcasted_iota(jnp.int32, (span, span), 1), 0.0, NEG)

    loads["q"].wait()
    loads["go"].wait()
    q_t[...] = q[...].T
    go_t[...] = go[...].T

    near = sorted(range(1, nz), key=lambda d: min(d, nz - d))
    for d in [0] + near:
        slot = kvrecv.at[c, zmod(-d)]
        if d:
            remote(slot, slot, kv_s.at[d], kv_r.at[d], at_z(zmod(d), c)).wait_recv()
        cp = remote(slot, slot, core_s.at[0, d], core_r.at[0, d], at_z(z, 1 - c))
        cp.start()
        sends.append(cp)
    pass_input(1)
    for d in [0] + near:
        slot = kvrecv.at[1 - c, zmod(-d)]
        remote(slot, slot, core_s.at[0, d], core_r.at[0, d], at_z(z, 1 - c)).wait_recv()

    half = nz * PR
    shalf = nz * SR
    for cc in range(2):
        kr = kvrecv[cc, :, 0:PR, :].reshape(half, HD).astype(F32)
        lo = cc * half
        kr = kr * cos[lo : lo + half, :] + swap_halves(kr) * sin[lo : lo + half, :]
        key[lo : lo + half, :] = kr.astype(BF16)
        val[lo : lo + half, :] = kvrecv[cc, :, PR : 2 * PR, :].reshape(half, HD)
        both = kvrecv[cc, :, 2 * PR : 2 * PR + 2 * SR, :].astype(F32)
        kr = both[:, 0:SR, :].reshape(shalf, HD)
        lo = past + cc * shalf
        kr = kr * cos[lo : lo + shalf, :] + swap_halves(kr) * sin[lo : lo + shalf, :]
        key[lo : lo + shalf, :] = kr.astype(BF16)
        val[lo : lo + shalf, :] = both[:, SR:, :].reshape(shalf, HD).astype(BF16)
    key_t[...] = key[...].T

    scale = HD**-0.5
    dk[...] = jnp.zeros_like(dk)
    dv[...] = jnp.zeros_like(dv)

    def one_head(h, carry):
        at = pl.ds(pl.multiple_of(h * HD, HD), HD)
        s = dot(key[...], q_t[at, :]) * scale + bias[...]
        e = jnp.exp(s - jnp.max(s, axis=0, keepdims=True))
        a = e * (1.0 / jnp.sum(e, axis=0, keepdims=True))
        ab = a.astype(BF16)
        dp = dot(val[...], go_t[at, :])
        delta = jnp.sum(ab.astype(F32) * dp, axis=0, keepdims=True)
        ds = (a * (dp - delta)).astype(BF16)
        qg[:, at] = (dot(key_t[...], ds) * scale).T.astype(BF16)
        dk[...] += dot(ds, q[:, at])
        dv[...] += dot(ab, go[:, at])
        return carry

    lax.fori_loop(0, QH, one_head, 0)

    g = dk[...] * scale
    dk[...] = g * cos[...] - swap_halves(g) * sin[...]
    sq, pq = span // 8, past // 4
    for j in range(4):
        for kv, acc in enumerate((dk, dv)):
            for hf in range(2):
                at = past + (2 * j + hf) * sq
                spart[hf, j, kv] = acc[at : at + sq, :].astype(BF16)
    mates = ((z, 1 - c, zp), (zx, c, 1 - zp), (zx, 1 - c, 1 - zp))

    def to_mates(i, part, recv):
        for k, (mz, mc, mp) in enumerate(mates):
            cp = remote(part.at[mc * 2 + mp], recv.at[k], grp_s.at[i, k], grp_r.at[i, k], at_z(mz, mc))
            cp.start()
            sends.append(cp)

    mine = c * 2 + zp

    def group_sum(i, part, recv):
        for k, (mz, mc, mp) in enumerate(mates):
            remote(recv.at[k], recv.at[k], grp_s.at[i, k], grp_r.at[i, k], at_z(mz, mc)).wait_recv()
        total = part[mine].astype(F32)
        for k in range(3):
            total = total + recv[k].astype(F32)
        return total.astype(BF16)

    for hf in range(2):
        to_mates(hf, spart.at[hf], srecv.at[hf])
    for j in range(4):
        for kv, acc in enumerate((dk, dv)):
            ppart[j, kv] = acc[j * pq : (j + 1) * pq, :].astype(BF16)
    pass_input(2)

    first, then = GATHER[nz]

    def ring(hf, d, e):
        slot, k = sg_all.at[hf, c, zmod(-d)], (d + e) % nz
        cp = remote(slot, slot, ag_s.at[hf, k], ag_r.at[hf, k], at_z(zmod(e), c))
        cp.start()
        sends.append(cp)

    def landed(hf, d):
        slot = sg_all.at[hf, c, zmod(-d)]
        remote(slot, slot, ag_s.at[hf, d], ag_r.at[hf, d], at_z(zmod(d), c)).wait_recv()

    def over_y(hf, d):
        zo = zmod(-d)
        src, dst = sg_all.at[hf, c, zo], dw_all.at[hf, c, y, lax.rem(zo, 2)]
        return zo // 2, remote(src, dst, yx_s.at[hf, d], yx_r.at[hf, y, lax.rem(zo, 2)], {"dp": zo // 2})

    def pass_on(hf, d):
        zo = zmod(-d)
        slot = sg_all.at[hf, c, zo]
        cp = remote(slot, slot, core_s.at[1 + hf, d], core_r.at[1 + hf, d], at_z(z, 1 - c))
        cp.start()
        sends.append(cp)
        there, yc = over_y(hf, d)

        @pl.when(there != y)
        def _():
            yc.start()

        @pl.when(there == y)
        def _():
            dw_all[hf, c, y, lax.rem(zo, 2)] = sg_all[hf, c, zo]

    for hf in range(2):
        sg_all[hf, c, z] = group_sum(hf, spart.at[hf], srecv.at[hf])
        for d in first:
            ring(hf, 0, d)
        pass_on(hf, 0)
    done = []
    for hf in range(2):
        for d, onward in then:
            landed(hf, d % nz)
            for e in onward:
                ring(hf, d % nz, e)
            pass_on(hf, d % nz)
            done.append((hf, d % nz))
    to_mates(2, ppart, precv)
    pass_input(3)
    for hf in range(2):
        for d in first:
            if (hf, d % nz) not in done:
                landed(hf, d % nz)
                pass_on(hf, d % nz)
                done.append((hf, d % nz))

    def own_copy(k):
        return remote(pout.at[k], powner.at[head], own_s.at[k], own_r.at[head], at_z(zp * (nz // 2) + k, c))

    def past_rows():
        total = group_sum(2, ppart, precv)
        for k in range(nz // 2):
            pout[k] = total[:, k * PR : (k + 1) * PR, :]

        for k in range(nz // 2):
            there = zp * (nz // 2) + k

            @pl.when(there != z)
            def _():
                own_copy(k).start()

            @pl.when(there == z)
            def _():
                powner[head] = pout[k]

    loads["kw"].wait()
    loads["vw"].wait()
    wide = heads * HD
    x_copies = []
    order = sorted(range(1, nz), key=lambda d: min(d, nz - d))
    for hf in range(2):
        for d in order:
            if (hf, d) not in done:
                landed(hf, d)
                pass_on(hf, d)
        for d in range(nz):
            slot = sg_all.at[hf, 1 - c, zmod(-d)]
            remote(slot, slot, core_s.at[1 + hf, d], core_r.at[1 + hf, d], at_z(z, 1 - c)).wait_recv()
        for h in range(heads):
            for cc in range(2):
                for p in range(2):
                    at = (cc * 2 + p) * sq
                    for kv in range(2):
                        col = (kv * heads + h) * HD
                        x_lhs[hf, at : at + sq, col : col + HD] = sg_all[hf, cc, 2 * h + p, kv]
        dx[...] = dot(x_lhs[hf, :, 0:wide], kw[...], 1, 1)
        total = (dx[...] + dot(x_lhs[hf, :, wide:], vw[...], 1, 1)).reshape(2, nz // 2, SR, 512)
        total = jnp.stack([total[0], total[1]], axis=1).reshape(2, span // 4, 512).astype(BF16)
        dxb[hf] = total
        x_copy = remote(dxb.at[hf], sg_o.at[:, hf], x_s.at[hf], x_r.at[hf], {"pipe": lax.rem(pipe + nx - 1, nx)})
        x_copies.append(x_copy)
        if nx > 1:
            pl.when(pipe > 0)(x_copy.start)
        if hf == 0:
            past_rows()

    def sequence_here(hf, d):
        b = ymod(-d)
        slot = dw_all.at[hf, c, b]
        if d > 0:
            for p in range(2):
                part = slot.at[p]
                remote(part, part, yx_s.at[hf, 0], yx_r.at[hf, b, p], {"dp": ymod(d)}).wait_recv()
        cp = remote(slot, slot, yc_s.at[hf, d], yc_r.at[hf, d], at_z(z, 1 - c))
        cp.start()
        sends.append(cp)

    def add_sequence(d, begin):
        b = ymod(-d)
        for hf in range(2):
            slot = dw_all.at[hf, 1 - c, b]
            remote(slot, slot, yc_s.at[hf, d], yc_r.at[hf, d], at_z(z, 1 - c)).wait_recv()
        for hf in range(2):
            for cc in range(2):
                for p in range(2):
                    at = (hf * 4 + cc * 2 + p) * sq
                    for kv in range(2):
                        w_rhs[at : at + sq, kv * HD : (kv + 1) * HD] = dw_all[hf, cc, b, p, kv]
        part = dot(n_t[b], w_rhs[...]).astype(BF16).astype(F32)
        dwk[...] = part[:, 0:HD] if begin else dwk[...] + part[:, 0:HD]
        dwv[...] = part[:, HD:] if begin else dwv[...] + part[:, HD:]

    turns = sorted(range(ny), key=lambda d: min(d, ny - d))
    for d in turns:
        sequence_here(0, d)
    ahead = ny // 2
    for i, d in enumerate(turns):
        sequence_here(1, d)
        if i >= ahead:
            add_sequence(turns[i - ahead], i == ahead)
    pass_input(ny // 2)
    for d in turns[ny - ahead :]:
        add_sequence(d, False)

    for h in range(heads):
        there = 2 * h + z // (nz // 2)

        @pl.when(there != z)
        def _():
            remote(powner.at[h], powner.at[h], own_s.at[0], own_r.at[h], at_z(there, c)).wait_recv()

    for h in range(heads):
        pkg[:, h * HD : (h + 1) * HD] = powner[h, 0].astype(F32)
        pvg[:, h * HD : (h + 1) * HD] = powner[h, 1].astype(F32)

    for hf in range(2):
        for d in range(nz):
            there, yc = over_y(hf, d)
            pl.when(there != y)(yc.wait_send)
    for k in range(nz // 2):

        @pl.when(zp * (nz // 2) + k != z)
        def _():
            own_copy(k).wait_send()

    for cp in sends:
        cp.wait_send()
    if nx > 1:
        for x_copy in x_copies:
            pl.when(pipe < nx - 1)(x_copy.wait_recv)
            pl.when(pipe > 0)(x_copy.wait_send)

    @pl.when(pipe == nx - 1)
    def _():
        sg_o[...] = jnp.zeros_like(sg_o)


def finish(*refs):
    copies = [pltpu.make_async_copy(a, b, refs[12].at[i]) for i, (a, b) in enumerate(zip(refs[:6], refs[6:12]))]
    for cp in copies:
        cp.start()
    for cp in copies:
        cp.wait()


def on_device(sizes, queries, grad_out, past_keys, past_values, span_keys, span_values, normed,
              key_weight, value_weight, offsets):
    nz, ny, nx = sizes
    heads = nz // 2
    past, span = nz * 2 * PR, nz * 2 * SR
    keys = past + span
    wide = heads * HD
    sq, pq = span // 8, past // 4
    any_ = pl.BlockSpec(memory_space=pltpu.HBM)
    vm = pltpu.VMEM
    dma = pltpu.SemaphoreType.DMA
    outs = pl.pallas_call(
        functools.partial(kernel, nz, ny, nx),
        name="gqa_backward",
        out_shape=(
            vm((span, QH * HD), BF16), vm((PR, wide), F32), vm((PR, wide), F32),
            vm((512, HD), F32), vm((512, HD), F32), vm((2, 2, span // 4, 512), BF16),
        ),
        in_specs=[pl.BlockSpec(memory_space=pltpu.SMEM)] + [any_] * 9,
        out_specs=(pl.BlockSpec(memory_space=pltpu.VMEM),) * 6,
        scratch_shapes=[
            vm((span, 512), BF16), vm((span, 512), BF16), vm((span, 512), BF16),
            vm((PR, wide), BF16), vm((PR, wide), BF16), vm((SR, wide), BF16), vm((SR, wide), BF16),
            vm((512, wide), BF16), vm((512, wide), BF16),
            vm((heads, 48, HD), BF16), vm((2, nz, 48, HD), BF16),
            vm((keys, HD), F32), vm((keys, HD), F32), vm((keys, span), F32),
            vm((keys, HD), BF16), vm((HD, keys), BF16), vm((keys, HD), BF16),
            vm((512, span), BF16), vm((512, span), BF16), vm((ny, 512, span), BF16),
            vm((keys, HD), F32), vm((keys, HD), F32),
            vm((2, 4, 2, sq, HD), BF16), vm((2, 3, 2, sq, HD), BF16),
            vm((4, 2, pq, HD), BF16), vm((3, 2, pq, HD), BF16),
            vm((nz // 2, 2, PR, HD), BF16), vm((heads, 2, PR, HD), BF16),
            vm((2, 2, nz, 2, sq, HD), BF16), vm((2, 2, ny, 2, 2, sq, HD), BF16),
            vm((2, span // 2, 2 * wide), BF16), vm((span // 2, 512), F32), vm((2, 2, span // 4, 512), BF16),
            vm((span, 2 * HD), BF16),
            dma((9,)), dma((nz,)), dma((nz,)), dma((3, nz)), dma((3, nz)),
            dma((3, 3)), dma((3, 3)), dma((2, nz)), dma((2, nz)), dma((nz // 2,)), dma((heads,)),
            dma((2, ny)), dma((2, ny)), dma((2, nz)), dma((2, ny, 2)), dma((2, ny)), dma((2, ny)), dma((2,)), dma((2,)),
        ],
        compiler_params=pltpu.CompilerParams(
            collective_id=0, has_side_effects=True, vmem_limit_bytes=67043328 - (3 << 19)
        ),
    )(
        offsets, queries[0, 0], grad_out[0, 0], normed[0, 0], past_keys[0, 0], past_values[0, 0],
        span_keys[0, 0], span_values[0, 0], key_weight[0], value_weight[0],
    )
    outs = pl.pallas_call(
        finish,
        name="finish",
        out_shape=tuple(jax.ShapeDtypeStruct(o.shape, o.dtype) for o in outs),
        in_specs=[pl.BlockSpec(memory_space=pl.ANY)] * 6,
        out_specs=(pl.BlockSpec(memory_space=pltpu.HBM),) * 6,
        scratch_shapes=[dma((6,))],
        compiler_params=pltpu.CompilerParams(vmem_limit_bytes=1 << 20),
    )(*outs)
    qg, pkg, pvg, kwg, vwg, sg = outs
    return (qg[None, None], pkg[None, None], pvg[None, None], kwg[None], vwg[None], sg.reshape(1, 1, span, 512))


def solution(mesh):
    sizes = (mesh.shape["tensor"] // 2, mesh.shape["dp"], mesh.shape["pipe"])
    rows = P("pipe", "dp", "tensor", None)
    cols = P("pipe", "dp", None, "tensor")
    weight = P("pipe", "tensor", None)
    return jax.shard_map(
        functools.partial(on_device, sizes),
        mesh=mesh,
        in_specs=(cols, cols, rows, rows, rows, rows, cols, weight, weight, P("pipe", "dp")),
        out_specs=(cols, rows, rows, P("pipe", "tensor", "dp"), P("pipe", "tensor", "dp"), cols),
        check_vma=False,
    )
```
